128 devices in a mesh: section: 8 (over x, core), expert: 16 (over z, y).
Axes of the slice: x: 4, y: 4, z: 4, core: 2. Of those that a mesh axis runs over, the one named last changes fastest.
Arguments:
- sent_acts: bfloat16 [8, 2048, 6144], P('section', 'expert'), may hold values from -6 to 6
- sent_cots: bfloat16 [8, 2048, 6144], P('section', 'expert'), may hold values from -6 to 6
- expert_ids: int32 [8, 2048, 2], P('section', 'expert'), may hold values from 0 to 7, as said below
- gate_probs: float32 [8, 2048, 2], P('section', 'expert'), may hold values from 0.1 to 0.9
- gate_weight: bfloat16 [8, 6144, 8192], P('section', None, 'expert'), may hold values from -0.078125 to 0.078125
- up_weight: bfloat16 [8, 6144, 8192], P('section', None, 'expert'), may hold values from -0.078125 to 0.078125
- down_weight: bfloat16 [8, 8192, 6144], P('section', 'expert'), may hold values from -0.0625 to 0.0625
Outputs:
- out_acts: bfloat16 [8, 2048, 6144], P('section', 'expert')
- in_grads: bfloat16 [8, 2048, 6144], P('section', 'expert')
The draws below stay inside these ranges and needn't reach their ends.
Inputs may be any that keep to these rules, and one draw needn't show every extreme that they name: `expert_ids`: in every section, at most 40 of the 128 tokens of one device name expert 0, and at least one device's tokens name it 40 times; a token's two experts differ.
All inputs are finite; a program needn't handle non-finite values.
Results may differ from the reference program's by a relative error of at most 0.015.
Values may be sent and summed in bfloat16 or wider, within the bound.
A program may use at most 128 MiB of HBM per device.

```python
import jax
import jax.numpy as jnp
from jax import lax

D = 6144
EXPERTS = 8
FW = 8192
TOK_DEV = 128
CAP = 40
SECTIONS = 8
TOKENS = 2048
N_EXPERT = 16


def draw_expert_ids(key, part):
    keys = jax.random.split(key, 7)
    lead = (SECTIONS, N_EXPERT)
    every = (SECTIONS, N_EXPERT, TOK_DEV)
    counts = jax.random.randint(keys[0], lead, CAP // 2, CAP + 1)
    full_at = jax.random.randint(keys[1], (SECTIONS, 1), 0, N_EXPERT)
    counts = jnp.where(jnp.arange(N_EXPERT, dtype=jnp.int32)[None, :] == full_at, CAP, counts)
    scores = jax.random.randint(keys[2], every, 0, 2 ** 20) * TOK_DEV + jnp.arange(TOK_DEV, dtype=jnp.int32)
    order = jnp.argsort(jnp.argsort(scores, axis=-1, stable=True), axis=-1, stable=True)
    chosen = order < counts[:, :, None]
    side = jax.random.randint(keys[3], every, 0, 2)
    other = jax.random.randint(keys[4], every, 1, EXPERTS)
    first = jax.random.randint(keys[5], every, 1, EXPERTS)
    step_by = jax.random.randint(keys[6], every, 1, EXPERTS - 1)
    second = 1 + (first - 1 + step_by) % (EXPERTS - 1)
    zero = jnp.zeros_like(other)
    left = jnp.where(chosen, jnp.where(side == 0, zero, other), first)
    right = jnp.where(chosen, jnp.where(side == 0, other, zero), second)
    return jnp.stack([left, right], axis=-1).reshape(SECTIONS, N_EXPERT * TOK_DEV, 2).astype(jnp.int32)


def level_of(stream_key, shape, shards, smallest, top_value):
    gain, own = 1.0, jax.random.fold_in(stream_key, 6)
    for position, blocks in shards:
        draws = jnp.exp(jax.random.uniform(jax.random.fold_in(own, position), (blocks,), jnp.float32, smallest / len(shards), top_value / len(shards)))
        gain = gain * jnp.repeat(draws, shape[position] // blocks).reshape([-1 if axis == position else 1 for axis in range(len(shape))])
    return gain


def gaussian(rng, extent, scale, reach, cuts=(), kind=jnp.bfloat16):
    array = jax.random.normal(rng, extent, jnp.float32) * scale
    if len(cuts) > 0:
        array = level_of(rng, extent, cuts, -0.22, 0.18) * array
    return jnp.clip(array, min=-reach, max=reach).astype(kind)


def setup_inputs(seed: int = 0) -> dict:
    splits = jax.random.split(jax.random.key(seed), 8)
    sent_acts = gaussian(splits[0], (SECTIONS, TOKENS, D), 1.0, 6.0, ((0, 8), (1, 16)))
    sent_cots = gaussian(splits[1], (SECTIONS, TOKENS, D), 1.0, 6.0, ((0, 8), (1, 16)))
    expert_ids = draw_expert_ids(jax.random.fold_in(splits[7], 71), 0)
    gate_probs = jnp.clip(0.1 + 0.79999997 * jax.random.uniform(splits[3], (SECTIONS, TOKENS, 2), jnp.float32) ** level_of(splits[3], (SECTIONS, TOKENS, 2), ((0, 8), (1, 16)), -0.2, 0.2), 0.1, 0.9)
    gate_weight = gaussian(splits[4], (SECTIONS, D, FW), D ** -0.5, 0.078125, ((0, 8), (2, 16)))
    up_weight = gaussian(splits[5], (SECTIONS, D, FW), D ** -0.5, 0.078125, ((0, 8), (2, 16)))
    down_weight = gaussian(splits[6], (SECTIONS, FW, D), FW ** -0.5, 0.0625, ((0, 8), (1, 16)))
    return dict(sent_acts=sent_acts, sent_cots=sent_cots, expert_ids=expert_ids, gate_probs=gate_probs, gate_weight=gate_weight, up_weight=up_weight, down_weight=down_weight)


def parts_sum(pieces):
    total = None
    for piece in pieces:
        value = lax.optimization_barrier(piece.astype(jnp.bfloat16)).astype(jnp.float32)
        total = value if total is None else total + value
    return total

def silu_grad(pre):
    sigma = jax.nn.sigmoid(pre)
    return sigma * (1.0 + pre * (1.0 - sigma))

def section_window(incoming, cot_in, routed, probs, gate_cols, up_cols, down_rows):
    part_width = FW // N_EXPERT
    tok_total = N_EXPERT * TOK_DEV
    slots_all = N_EXPERT * CAP
    chosen = routed == 0
    picked = jnp.any(chosen, axis=1)
    picked_int = picked.astype(jnp.int32)
    share = lax.optimization_barrier(jnp.sum(jnp.where(chosen, probs, jnp.zeros((), probs.dtype)), axis=1))
    blocks_int = picked_int.reshape(N_EXPERT, TOK_DEV)
    ranking = (jnp.cumsum(blocks_int, axis=1) - blocks_int).reshape(-1).astype(jnp.int32)
    owner = (jnp.arange(tok_total, dtype=jnp.int32) // TOK_DEV).astype(jnp.int32)
    slot_of = jnp.where(picked, owner * CAP + ranking, slots_all).astype(jnp.int32)
    table = jnp.full((slots_all + 1,), -1, jnp.int32).at[slot_of].set(jnp.arange(tok_total, dtype=jnp.int32))[:slots_all]
    filled = table >= 0
    source = jnp.maximum(table, 0).astype(jnp.int32)
    rows_in = jnp.where(filled[:, None], incoming[source], jnp.zeros((), incoming.dtype))
    out_grad = (cot_in.astype(jnp.float32) * share[:, None]).astype(jnp.bfloat16)
    rows_grad = jnp.where(filled[:, None], out_grad[source], jnp.zeros((), out_grad.dtype))
    pre_gate = jnp.dot(rows_in, gate_cols, preferred_element_type=jnp.float32)
    pre_up = jnp.dot(rows_in, up_cols, preferred_element_type=jnp.float32)
    hidden = (jax.nn.silu(pre_gate) * pre_up).astype(jnp.bfloat16)
    expert_out = parts_sum([jnp.dot(hidden[:, offset:offset + part_width], down_rows[offset:offset + part_width], preferred_element_type=jnp.float32) for offset in range(0, FW, part_width)])
    hid_grad = jnp.dot(rows_grad, down_rows.T, preferred_element_type=jnp.float32)
    gate_grad = (hid_grad * pre_up * silu_grad(pre_gate)).astype(jnp.bfloat16)
    up_grad = (hid_grad * jax.nn.silu(pre_gate)).astype(jnp.bfloat16)
    back_rows = parts_sum([jnp.dot(gate_grad[:, offset:offset + part_width], gate_cols[:, offset:offset + part_width].T, preferred_element_type=jnp.float32) + jnp.dot(up_grad[:, offset:offset + part_width], up_cols[:, offset:offset + part_width].T, preferred_element_type=jnp.float32) for offset in range(0, FW, part_width)])
    back_index = jnp.minimum(slot_of, slots_all - 1).astype(jnp.int32)
    out_acts = jnp.where(picked[:, None], share[:, None] * expert_out[back_index], jnp.zeros((), expert_out.dtype)).astype(jnp.bfloat16)
    in_grads = jnp.where(picked[:, None], back_rows[back_index], jnp.zeros((), back_rows.dtype)).astype(jnp.bfloat16)
    return (out_acts, in_grads)

def reference(sent_acts, sent_cots, expert_ids, gate_probs, gate_weight, up_weight, down_weight):
    incoming = jnp.roll(sent_acts, 1, axis=0)
    cot_in = jnp.roll(sent_cots, -1, axis=0)
    out_acts, in_grads = lax.map(lambda packed_args: section_window(*packed_args), (incoming, cot_in, expert_ids, gate_probs, gate_weight, up_weight, down_weight))
    return (out_acts, in_grads)
```

```python
import functools

import jax
import jax.numpy as jnp
from jax import lax
from jax.experimental import pallas as pl
from jax.experimental.pallas import tpu as pltpu
from jax.sharding import PartitionSpec as P

CAP = 40
SIDE = 4
MESH = pl.DeviceIdType.MESH
F32 = jnp.float32
BF16 = jnp.bfloat16
HALVES = (0, 1)
PIECES = (0, 1)
CORNERS = ((0, 0), (1, 0), (0, 1), (1, 1))


def dot_nn(lhs, rhs):
    return lax.dot_general(lhs, rhs, (((1,), (0,)), ((), ())), preferred_element_type=F32)


def dot_nt(lhs, rhs):
    return lax.dot_general(lhs, rhs, (((1,), (1,)), ((), ())), preferred_element_type=F32)


class Place:
    def __init__(self, sections):
        self.sections = sections
        self.section = lax.axis_index("section")
        self.expert = lax.axis_index("expert")
        self.at = (self.expert // SIDE, self.expert % SIDE)

    def axis(self, half, phase):
        return 1 - half if phase == 1 else half

    def beside(self, axis, step):
        z, y = self.at
        if axis == 0:
            z = (z + step) % SIDE
        else:
            y = (y + step) % SIDE
        return (self.section, z * SIDE + y)

    def other_section(self, step):
        return ((self.section + step) % self.sections, self.expert)

    def outer(self, half):
        return self.at[half]

    def inner(self, half):
        return self.at[1 - half]


class Links:
    def __init__(self, send_sem, recv_sem):
        self.send_sem, self.recv_sem = send_sem, recv_sem
        self.used = 0

    def copy(self, src, dst, device):
        k = self.used
        self.used += 1
        return pltpu.make_async_remote_copy(
            src_ref=src,
            dst_ref=dst,
            send_sem=self.send_sem.at[k],
            recv_sem=self.recv_sem.at[k],
            device_id=device,
            device_id_type=MESH,
        )


class GatherRing:
    def __init__(self, place, links, half, phase, piece):
        axis = place.axis(half, phase)
        me = place.at[axis]
        plus, minus = place.beside(axis, 1), place.beside(axis, SIDE - 1)
        before, after = (me + SIDE - 1) % SIDE, (me + 1) % SIDE
        self.own = [
            [links.copy(piece(q, me), piece(q, me), device) for device in (plus, minus)]
            for q in PIECES
        ]
        self.passed = [
            links.copy(piece(0, before), piece(0, before), plus),
            links.copy(piece(1, after), piece(1, after), minus),
        ]

    def start(self, q):
        self.own[q][q].start()
        self.own[q][1 - q].start()

    def relay(self):
        for q in PIECES:
            self.own[q][q].wait_recv()
            self.passed[q].start()

    def finish(self):
        self.own[0][1].wait_recv()
        self.own[1][0].wait_recv()
        self.passed[0].wait_recv()
        self.passed[1].wait_recv()

    def wait_sends(self):
        for q in PIECES:
            for way in (0, 1):
                self.own[q][way].wait_send()
            self.passed[q].wait_send()


class ReduceRing:
    def __init__(self, place, links, half, phase, piece, through, landed):
        axis = place.axis(half, phase)
        me = place.at[axis]
        plus, minus = place.beside(axis, 1), place.beside(axis, SIDE - 1)
        before, after = (me + SIDE - 1) % SIDE, (me + 1) % SIDE
        opposite = (me + 2) % SIDE
        self.piece, self.me, self.through, self.landed = piece, me, through, landed
        self.next = (after, before)
        devices = (plus, minus)
        self.far = [links.copy(piece(q, opposite), through(q), devices[q]) for q in PIECES]
        self.near = [
            links.copy(piece(1 - q, self.next[q]), landed(q, 1 - q), devices[q]) for q in PIECES
        ]
        self.passed = [links.copy(through(q), landed(q, q), devices[q]) for q in PIECES]

    def start(self):
        for q in PIECES:
            self.far[q].start()
        for q in PIECES:
            self.near[q].start()

    def relay(self, add_into):
        for q in PIECES:
            self.far[q].wait_recv()
            add_into(self.through(q), self.piece(q, self.next[q]))
        for q in PIECES:
            self.passed[q].start()

    def finish(self):
        for q in PIECES:
            self.near[q].wait_recv()
            self.passed[q].wait_recv()

    def wait_sends(self):
        for q in PIECES:
            self.far[q].wait_send()
            self.near[q].wait_send()
            self.passed[q].wait_send()


def kernel(
    sections,
    acts_ref,
    cots_ref,
    ids_ref,
    probs_ref,
    gate_ref,
    up_ref,
    down_ref,
    out_ref,
    grad_ref,
    gate_w,
    up_w,
    down_w,
    info,
    rows_x,
    rows_g,
    part,
    pre_g,
    pre_u,
    hid,
    grad_g,
    grad_u,
    thru_big,
    land_big,
    thru_small,
    land_small,
    send_sem,
    recv_sem,
    load_sem,
    store_sem,
):
    place = Place(sections)
    links = Links(send_sem, recv_sem)
    toks, width = acts_ref.shape
    cols = width // 4
    units = gate_ref.shape[1]
    group = SIDE * CAP

    def span(h, q):
        return pl.ds((h * 2 + q) * cols, cols)

    barrier = pltpu.get_barrier_semaphore()
    around = [place.beside(axis, step) for axis in (0, 1) for step in (1, SIDE - 1)]
    around += [place.other_section(step) for step in (1, sections - 1)]
    for device in around:
        pl.semaphore_signal(barrier, inc=1, device_id=device, device_id_type=MESH)

    acts_here = down_w.at[pl.ds(0, toks)]
    cots_here = down_w.at[pl.ds(toks, toks)]
    load_acts = pltpu.make_async_copy(acts_ref, acts_here, load_sem.at[0])
    load_cots = pltpu.make_async_copy(cots_ref, cots_here, load_sem.at[1])
    load_gate = pltpu.make_async_copy(gate_ref, gate_w, load_sem.at[2])
    load_up = pltpu.make_async_copy(up_ref, up_w, load_sem.at[3])
    load_down = pltpu.make_async_copy(down_ref, down_w, load_sem.at[4])
    load_acts.start()
    load_cots.start()

    chosen = ids_ref[...] == 0
    flags = jnp.where(chosen, 1.0, 0.0).astype(F32)
    weights = jnp.where(chosen, probs_ref[...], 0.0)
    picked = jnp.broadcast_to(flags[0:1] + flags[1:2], (8, toks))
    share = jnp.broadcast_to(weights[0:1] + weights[1:2], (8, toks))
    earlier = lax.broadcasted_iota(jnp.int32, (toks, toks), 0) < lax.broadcasted_iota(
        jnp.int32, (toks, toks), 1
    )
    rank = dot_nn(picked.astype(BF16), jnp.where(earlier, 1.0, 0.0).astype(BF16))
    slot = jnp.where(picked > 0.5, rank, -1.0)
    line = lax.broadcasted_iota(jnp.int32, (8, toks), 0)
    info[0] = jnp.where(line == 0, slot, share)

    pl.semaphore_wait(barrier, len(around))
    info_back = links.copy(info.at[0], info.at[1], place.other_section(sections - 1))
    info_on = links.copy(info.at[0], info.at[2], place.other_section(1))
    info_back.start()
    info_on.start()

    def selection(block):
        slot_line = block[0:1, :]
        share_line = block[1:2, :]
        number = lax.broadcasted_iota(jnp.int32, (CAP, toks), 0).astype(F32)
        hit = number == slot_line
        pick = jnp.where(hit, 1.0, 0.0).astype(BF16)
        slot_share = jnp.sum(jnp.where(hit, share_line, 0.0), axis=1, keepdims=True)
        return pick, slot_share

    def own_slot(rows, h, q):
        return rows.at[h, q, place.outer(h), place.inner(h)]

    load_acts.wait()
    info_back.wait_recv()
    pick, _ = selection(info[1])
    send_x = {}
    for h, q in CORNERS:
        part[h, q, 0, 0] = dot_nn(pick, down_w[pl.ds(0, toks), span(h, q)]).astype(BF16)
        send_x[h, q] = links.copy(
            part.at[h, q, 0, 0], own_slot(rows_x, h, q), place.other_section(1)
        )
        send_x[h, q].start()

    load_cots.wait()
    info_on.wait_recv()
    pick, slot_share = selection(info[2])
    send_g = {}
    for h, q in CORNERS:
        chosen_rows = dot_nn(pick, down_w[pl.ds(toks, toks), span(h, q)])
        part[h, q, 0, 1] = (chosen_rows * slot_share).astype(BF16)
        send_g[h, q] = links.copy(
            part.at[h, q, 0, 1], own_slot(rows_g, h, q), place.other_section(sections - 1)
        )
        send_g[h, q].start()

    load_gate.start()
    load_up.start()
    load_down.start()

    def gathers(rows):
        first = [
            GatherRing(place, links, h, 1, lambda q, j, h=h: rows.at[h, q, place.outer(h), j])
            for h in HALVES
        ]
        second = [
            GatherRing(place, links, h, 2, lambda q, j, h=h: rows.at[h, q, j]) for h in HALVES
        ]
        return first, second

    first_x, second_x = gathers(rows_x)
    first_g, second_g = gathers(rows_g)

    for h, q in CORNERS:
        send_x[h, q].wait_recv()
        first_x[h].start(q)
    for h, q in CORNERS:
        send_g[h, q].wait_recv()
        first_g[h].start(q)
    for h in HALVES:
        first_x[h].relay()
    for h in HALVES:
        first_x[h].finish()
        for q in PIECES:
            second_x[h].start(q)
    for h in HALVES:
        first_g[h].relay()
    for h in HALVES:
        first_g[h].finish()
        for q in PIECES:
            second_g[h].start(q)
    for h in HALVES:
        second_x[h].relay()
    for h in HALVES:
        second_x[h].finish()

    def block_rows(rows, h, q, z):
        value = rows[h, q, z] if h == 0 else rows[h, q, :, z]
        return value.reshape(group, cols)

    def put_rows(rows, h, q, z, value):
        value = value.astype(BF16).reshape(SIDE, CAP, cols)
        if h == 0:
            rows[h, q, z] = value
        else:
            rows[h, q, :, z] = value

    load_gate.wait()
    load_up.wait()

    def project(z, carry):
        here = pl.ds(pl.multiple_of(z * group, group), group)
        total_g = jnp.zeros((group, units), F32)
        total_u = jnp.zeros((group, units), F32)
        for h, q in CORNERS:
            block = block_rows(rows_x, h, q, z)
            total_g += dot_nn(block, gate_w[span(h, q), :])
            total_u += dot_nn(block, up_w[span(h, q), :])
        pre_g[here, :] = total_g
        pre_u[here, :] = total_u
        hid[here, :] = (total_g * jax.nn.sigmoid(total_g) * total_u).astype(BF16)
        return carry

    lax.fori_loop(0, SIDE, project, 0)

    for h in HALVES:
        second_g[h].relay()

    load_down.wait()
    for h, q in CORNERS:
        send_x[h, q].wait_send()
        send_g[h, q].wait_send()

    def forward_terms(z, carry):
        here = pl.ds(pl.multiple_of(z * group, group), group)
        units_here = hid[here, :]
        for h, q in CORNERS:
            put_rows(part, h, q, z, dot_nn(units_here, down_w[:, span(h, q)]))
        return carry

    lax.fori_loop(0, SIDE, forward_terms, 0)

    def reduces(rows, which):
        first = [
            ReduceRing(
                place,
                links,
                h,
                2,
                lambda q, j, h=h: rows.at[h, q, j],
                lambda q, h=h: thru_big.at[which, h, q],
                lambda way, q, h=h: land_big.at[which, h, way, q],
            )
            for h in HALVES
        ]
        second = [
            ReduceRing(
                place,
                links,
                h,
                1,
                lambda q, j, h=h: rows.at[h, q, place.outer(h), j],
                lambda q, h=h: thru_small.at[which, h, q],
                lambda way, q, h=h: land_small.at[which, h, way, q],
            )
            for h in HALVES
        ]
        return first, second

    def add_big(into, term):
        def step(j, carry):
            into[j] = (into[j].astype(F32) + term[j].astype(F32)).astype(BF16)
            return carry

        lax.fori_loop(0, SIDE, step, 0)

    def add_small(into, term):
        into[...] = (into[...].astype(F32) + term[...].astype(F32)).astype(BF16)

    def close_first(rows, which, h):
        mine = place.outer(h)

        def step(j, carry):
            for q in PIECES:
                total = rows[h, q, mine, j].astype(F32)
                for way in (0, 1):
                    total += land_big[which, h, way, q, j].astype(F32)
                rows[h, q, mine, j] = total.astype(BF16)
            return carry

        lax.fori_loop(0, SIDE, step, 0)

    first_o, second_o = reduces(part, 0)
    first_b, second_b = reduces(rows_x, 1)

    for h in HALVES:
        first_o[h].start()

    for h in HALVES:
        second_g[h].finish()

    def unit_grads(z, carry):
        here = pl.ds(pl.multiple_of(z * group, group), group)
        hidden_grad = jnp.zeros((group, units), F32)
        for h, q in CORNERS:
            hidden_grad += dot_nt(block_rows(rows_g, h, q, z), down_w[:, span(h, q)])
        gate = pre_g[here, :]
        sigma = jax.nn.sigmoid(gate)
        grad_g[here, :] = (
            hidden_grad * pre_u[here, :] * (sigma * (1.0 + gate * (1.0 - sigma)))
        ).astype(BF16)
        grad_u[here, :] = (hidden_grad * (gate * sigma)).astype(BF16)
        return carry

    lax.fori_loop(0, SIDE, unit_grads, 0)

    for h in HALVES:
        first_o[h].relay(add_big)

    for rings in (first_x, second_x):
        for h in HALVES:
            rings[h].wait_sends()

    def backward_terms(z, carry):
        here = pl.ds(pl.multiple_of(z * group, group), group)
        gate_here, up_here = grad_g[here, :], grad_u[here, :]
        for h, q in CORNERS:
            term = dot_nt(gate_here, gate_w[span(h, q), :])
            put_rows(rows_x, h, q, z, term + dot_nt(up_here, up_w[span(h, q), :]))
        return carry

    lax.fori_loop(0, SIDE, backward_terms, 0)

    for h in HALVES:
        first_b[h].start()

    local_pick, local_share = selection(info[0])

    def close_second(rows, which, h, q, staged):
        total = rows[h, q, place.outer(h), place.inner(h)].astype(F32)
        for way in (0, 1):
            total += land_small[which, h, way, q].astype(F32)
        if which == 0:
            total = total * local_share
        spread = lax.dot_general(
            local_pick, total.astype(BF16), (((0,), (0,)), ((), ())), preferred_element_type=F32
        )
        down_w[pl.ds(staged, toks), span(h, q)] = spread.astype(BF16)

    def close(rows, which, first, second):
        staged = which * toks
        for h in HALVES:
            second[h].relay(add_small)
        for h in HALVES:
            second[h].finish()
            for q in PIECES:
                close_second(rows, which, h, q, staged)

    for h in HALVES:
        first_o[h].finish()
        close_first(part, 0, h)
        second_o[h].start()
    for h in HALVES:
        first_b[h].relay(add_big)
    close(part, 0, first_o, second_o)
    store_out = pltpu.make_async_copy(acts_here, out_ref, store_sem.at[0])
    store_out.start()
    for h in HALVES:
        first_b[h].finish()
        close_first(rows_x, 1, h)
        second_b[h].start()
    close(rows_x, 1, first_b, second_b)
    store_grad = pltpu.make_async_copy(cots_here, grad_ref, store_sem.at[1])
    store_grad.start()

    info_back.wait_send()
    info_on.wait_send()
    for rings in (first_g, second_g, first_o, second_o, first_b, second_b):
        for h in HALVES:
            rings[h].wait_sends()
    store_out.wait()
    store_grad.wait()
    assert links.used == COPIES


COPIES = 2 + 8 + 2 * 4 * 6 + 2 * 4 * 6


def body(sections, sent_acts, sent_cots, expert_ids, gate_probs, gate_weight, up_weight, down_weight):
    acts, cots = sent_acts[0], sent_cots[0]
    ids, probs = expert_ids[0].T, gate_probs[0].T
    toks, width = acts.shape
    cols = width // 4
    units = gate_weight.shape[2]
    rows = SIDE * SIDE * CAP
    hbm = pl.BlockSpec(memory_space=pl.ANY)
    vmem = pl.BlockSpec(memory_space=pltpu.VMEM)
    block = (CAP, cols)
    out_acts, in_grads = pl.pallas_call(
        functools.partial(kernel, sections),
        out_shape=(
            jax.ShapeDtypeStruct((toks, width), BF16),
            jax.ShapeDtypeStruct((toks, width), BF16),
        ),
        in_specs=[hbm, hbm, vmem, vmem, hbm, hbm, hbm],
        out_specs=(hbm, hbm),
        scratch_shapes=[
            pltpu.VMEM((width, units), BF16),
            pltpu.VMEM((width, units), BF16),
            pltpu.VMEM((units, width), BF16),
            pltpu.VMEM((3, 8, toks), F32),
            pltpu.VMEM((2, 2, SIDE, SIDE) + block, BF16),
            pltpu.VMEM((2, 2, SIDE, SIDE) + block, BF16),
            pltpu.VMEM((2, 2, SIDE, SIDE) + block, BF16),
            pltpu.VMEM((rows, units), F32),
            pltpu.VMEM((rows, units), F32),
            pltpu.VMEM((rows, units), BF16),
            pltpu.VMEM((rows, units), BF16),
            pltpu.VMEM((rows, units), BF16),
            pltpu.VMEM((2, 2, 2, SIDE) + block, BF16),
            pltpu.VMEM((2, 2, 2, 2, SIDE) + block, BF16),
            pltpu.VMEM((2, 2, 2) + block, BF16),
            pltpu.VMEM((2, 2, 2, 2) + block, BF16),
            pltpu.SemaphoreType.DMA((COPIES,)),
            pltpu.SemaphoreType.DMA((COPIES,)),
            pltpu.SemaphoreType.DMA((5,)),
            pltpu.SemaphoreType.DMA((2,)),
        ],
        compiler_params=pltpu.CompilerParams(
            collective_id=0, has_side_effects=True, vmem_limit_bytes=67043328
        ),
    )(acts, cots, ids, probs, gate_weight[0], up_weight[0], down_weight[0])
    return (out_acts[None], in_grads[None])


def solution(mesh):
    placed = (
        P("section", "expert", None),
        P("section", "expert", None),
        P("section", "expert", None),
        P("section", "expert", None),
        P("section", None, "expert"),
        P("section", None, "expert"),
        P("section", "expert", None),
    )
    return jax.shard_map(
        functools.partial(body, mesh.shape["section"]),
        mesh=mesh,
        in_specs=placed,
        out_specs=(P("section", "expert", None), P("section", "expert", None)),
        check_vma=False,
    )
```

```python
import functools

import jax
import jax.numpy as jnp
from jax import lax
from jax.experimental import pallas as pl
from jax.experimental.pallas import tpu as pltpu
from jax.sharding import PartitionSpec as P

CAP = 40
SIDE = 4
MESH = pl.DeviceIdType.MESH
F32 = jnp.float32
BF16 = jnp.bfloat16
HALVES = (0, 1)
PIECES = (0, 1)
CORNERS = ((0, 0), (1, 0), (0, 1), (1, 1))


def dot_nn(lhs, rhs):
    return lax.dot_general(lhs, rhs, (((1,), (0,)), ((), ())), preferred_element_type=F32)


def dot_nt(lhs, rhs):
    return lax.dot_general(lhs, rhs, (((1,), (1,)), ((), ())), preferred_element_type=F32)


class Place:
    def __init__(self, sections):
        self.sections = sections
        self.section = lax.axis_index("section")
        self.expert = lax.axis_index("expert")
        self.at = (self.expert // SIDE, self.expert % SIDE)

    def axis(self, half, phase):
        return 1 - half if phase == 1 else half

    def beside(self, axis, step):
        z, y = self.at
        if axis == 0:
            z = (z + step) % SIDE
        else:
            y = (y + step) % SIDE
        return (self.section, z * SIDE + y)

    def other_section(self, step):
        return ((self.section + step) % self.sections, self.expert)

    def outer(self, half):
        return self.at[half]

    def inner(self, half):
        return self.at[1 - half]


class Links:
    def __init__(self, send_sem, recv_sem):
        self.send_sem, self.recv_sem = send_sem, recv_sem
        self.used = 0

    def copy(self, src, dst, device):
        k = self.used
        self.used += 1
        return pltpu.make_async_remote_copy(
            src_ref=src,
            dst_ref=dst,
            send_sem=self.send_sem.at[k],
            recv_sem=self.recv_sem.at[k],
            device_id=device,
            device_id_type=MESH,
        )


class GatherRing:
    def __init__(self, place, links, half, phase, piece):
        axis = place.axis(half, phase)
        me = place.at[axis]
        plus, minus = place.beside(axis, 1), place.beside(axis, SIDE - 1)
        before, after = (me + SIDE - 1) % SIDE, (me + 1) % SIDE
        self.own = [
            [links.copy(piece(q, me), piece(q, me), device) for device in (plus, minus)]
            for q in PIECES
        ]
        self.passed = [
            links.copy(piece(0, before), piece(0, before), plus),
            links.copy(piece(1, after), piece(1, after), minus),
        ]

    def start(self, q):
        self.own[q][q].start()
        self.own[q][1 - q].start()

    def relay(self):
        for q in PIECES:
            self.own[q][q].wait_recv()
            self.passed[q].start()

    def finish(self):
        self.own[0][1].wait_recv()
        self.own[1][0].wait_recv()
        self.passed[0].wait_recv()
        self.passed[1].wait_recv()

    def wait_sends(self):
        for q in PIECES:
            for way in (0, 1):
                self.own[q][way].wait_send()
            self.passed[q].wait_send()


class ReduceRing:
    def __init__(self, place, links, half, phase, piece, through, landed):
        axis = place.axis(half, phase)
        me = place.at[axis]
        plus, minus = place.beside(axis, 1), place.beside(axis, SIDE - 1)
        before, after = (me + SIDE - 1) % SIDE, (me + 1) % SIDE
        opposite = (me + 2) % SIDE
        self.piece, self.me, self.through, self.landed = piece, me, through, landed
        self.next = (after, before)
        devices = (plus, minus)
        self.far = [links.copy(piece(q, opposite), through(q), devices[q]) for q in PIECES]
        self.near = [
            links.copy(piece(1 - q, self.next[q]), landed(q, 1 - q), devices[q]) for q in PIECES
        ]
        self.passed = [links.copy(through(q), landed(q, q), devices[q]) for q in PIECES]

    def start_far(self):
        for q in PIECES:
            self.far[q].start()

    def start_near(self):
        for q in PIECES:
            self.near[q].start()

    def start(self):
        self.start_far()
        self.start_near()

    def relay(self, add_into):
        for q in PIECES:
            self.far[q].wait_recv()
            add_into(self.through(q), self.piece(q, self.next[q]))
        for q in PIECES:
            self.passed[q].start()

    def finish(self):
        for q in PIECES:
            self.near[q].wait_recv()
            self.passed[q].wait_recv()

    def wait_sends(self):
        for q in PIECES:
            self.far[q].wait_send()
            self.near[q].wait_send()
            self.passed[q].wait_send()


def kernel(
    sections,
    acts_ref,
    cots_ref,
    ids_ref,
    probs_ref,
    gate_ref,
    up_ref,
    down_ref,
    out_ref,
    grad_ref,
    gate_w,
    up_w,
    down_w,
    info,
    rows_x,
    rows_g,
    part,
    pre_g,
    pre_u,
    hid,
    grad_g,
    grad_u,
    thru_big,
    land_big,
    thru_small,
    land_small,
    send_sem,
    recv_sem,
    load_sem,
    store_sem,
):
    place = Place(sections)
    links = Links(send_sem, recv_sem)
    toks, width = acts_ref.shape
    cols = width // 4
    units = gate_ref.shape[1]
    group = SIDE * CAP

    def span(h, q):
        return pl.ds((h * 2 + q) * cols, cols)

    barrier = pltpu.get_barrier_semaphore()
    around = [place.beside(axis, step) for axis in (0, 1) for step in (1, SIDE - 1)]
    around += [place.other_section(step) for step in (1, sections - 1)]
    for device in around:
        pl.semaphore_signal(barrier, inc=1, device_id=device, device_id_type=MESH)

    acts_here = down_w.at[pl.ds(0, toks)]
    cots_here = down_w.at[pl.ds(toks, toks)]
    load_acts = pltpu.make_async_copy(acts_ref, acts_here, load_sem.at[0])
    load_cots = pltpu.make_async_copy(cots_ref, cots_here, load_sem.at[1])
    load_gate = pltpu.make_async_copy(gate_ref, gate_w, load_sem.at[2])
    load_up = pltpu.make_async_copy(up_ref, up_w, load_sem.at[3])
    load_down = pltpu.make_async_copy(down_ref, down_w, load_sem.at[4])
    load_acts.start()
    load_cots.start()

    chosen = ids_ref[...] == 0
    flags = jnp.where(chosen, 1.0, 0.0).astype(F32)
    weights = jnp.where(chosen, probs_ref[...], 0.0)
    picked = jnp.broadcast_to(flags[0:1] + flags[1:2], (8, toks))
    share = jnp.broadcast_to(weights[0:1] + weights[1:2], (8, toks))
    earlier = lax.broadcasted_iota(jnp.int32, (toks, toks), 0) < lax.broadcasted_iota(
        jnp.int32, (toks, toks), 1
    )
    rank = dot_nn(picked.astype(BF16), jnp.where(earlier, 1.0, 0.0).astype(BF16))
    slot = jnp.where(picked > 0.5, rank, -1.0)
    line = lax.broadcasted_iota(jnp.int32, (8, toks), 0)
    info[0] = jnp.where(line == 0, slot, share)

    pl.semaphore_wait(barrier, len(around))
    info_back = links.copy(info.at[0], info.at[1], place.other_section(sections - 1))
    info_on = links.copy(info.at[0], info.at[2], place.other_section(1))
    info_back.start()
    info_on.start()

    def selection(block):
        slot_line = block[0:1, :]
        share_line = block[1:2, :]
        number = lax.broadcasted_iota(jnp.int32, (CAP, toks), 0).astype(F32)
        hit = number == slot_line
        pick = jnp.where(hit, 1.0, 0.0).astype(BF16)
        slot_share = jnp.sum(jnp.where(hit, share_line, 0.0), axis=1, keepdims=True)
        return pick, slot_share

    def own_slot(rows, h, q):
        return rows.at[h, q, place.outer(h), place.inner(h)]

    load_acts.wait()
    info_back.wait_recv()
    pick, _ = selection(info[1])
    send_x = {}
    for h, q in CORNERS:
        part[h, q, 0, 0] = dot_nn(pick, down_w[pl.ds(0, toks), span(h, q)]).astype(BF16)
        send_x[h, q] = links.copy(
            part.at[h, q, 0, 0], own_slot(rows_x, h, q), place.other_section(1)
        )
        send_x[h, q].start()

    load_cots.wait()
    info_on.wait_recv()
    pick, slot_share = selection(info[2])
    send_g = {}
    for h, q in CORNERS:
        chosen_rows = dot_nn(pick, down_w[pl.ds(toks, toks), span(h, q)])
        part[h, q, 0, 1] = (chosen_rows * slot_share).astype(BF16)
        send_g[h, q] = links.copy(
            part.at[h, q, 0, 1], own_slot(rows_g, h, q), place.other_section(sections - 1)
        )
        send_g[h, q].start()

    load_gate.start()
    load_up.start()
    load_down.start()

    def gathers(rows):
        first = [
            GatherRing(place, links, h, 1, lambda q, j, h=h: rows.at[h, q, place.outer(h), j])
            for h in HALVES
        ]
        second = [
            GatherRing(place, links, h, 2, lambda q, j, h=h: rows.at[h, q, j]) for h in HALVES
        ]
        return first, second

    first_x, second_x = gathers(rows_x)
    first_g, second_g = gathers(rows_g)

    for h, q in CORNERS:
        send_x[h, q].wait_recv()
        first_x[h].start(q)
    for h, q in CORNERS:
        send_g[h, q].wait_recv()
        first_g[h].start(q)
    for h in HALVES:
        first_x[h].relay()
    for h in HALVES:
        first_x[h].finish()
        for q in PIECES:
            second_x[h].start(q)
    for h in HALVES:
        first_g[h].relay()
    for h in HALVES:
        second_x[h].relay()
    for h in HALVES:
        first_g[h].finish()
        for q in PIECES:
            second_g[h].start(q)
    for h in HALVES:
        second_x[h].finish()

    def block_rows(rows, h, q, z):
        value = rows[h, q, z] if h == 0 else rows[h, q, :, z]
        return value.reshape(group, cols)

    def put_rows(rows, h, q, z, value):
        value = value.astype(BF16).reshape(SIDE, CAP, cols)
        if h == 0:
            rows[h, q, z] = value
        else:
            rows[h, q, :, z] = value

    load_gate.wait()
    load_up.wait()

    def project(z, carry):
        here = pl.ds(pl.multiple_of(z * group, group), group)
        total_g = jnp.zeros((group, units), F32)
        total_u = jnp.zeros((group, units), F32)
        for h, q in CORNERS:
            block = block_rows(rows_x, h, q, z)
            total_g += dot_nn(block, gate_w[span(h, q), :])
            total_u += dot_nn(block, up_w[span(h, q), :])
        pre_g[here, :] = total_g
        pre_u[here, :] = total_u
        hid[here, :] = (total_g * jax.nn.sigmoid(total_g) * total_u).astype(BF16)
        return carry

    lax.fori_loop(0, SIDE, project, 0)

    for h in HALVES:
        second_g[h].relay()

    load_down.wait()
    for h, q in CORNERS:
        send_x[h, q].wait_send()
        send_g[h, q].wait_send()

    def forward_terms(z, carry):
        here = pl.ds(pl.multiple_of(z * group, group), group)
        units_here = hid[here, :]
        for h, q in CORNERS:
            put_rows(part, h, q, z, dot_nn(units_here, down_w[:, span(h, q)]))
        return carry

    lax.fori_loop(0, SIDE, forward_terms, 0)

    def reduces(rows, which):
        first = [
            ReduceRing(
                place,
                links,
                h,
                2,
                lambda q, j, h=h: rows.at[h, q, j],
                lambda q, h=h: thru_big.at[which, h, q],
                lambda way, q, h=h: land_big.at[which, h, way, q],
            )
            for h in HALVES
        ]
        second = [
            ReduceRing(
                place,
                links,
                h,
                1,
                lambda q, j, h=h: rows.at[h, q, place.outer(h), j],
                lambda q, h=h: thru_small.at[which, h, q],
                lambda way, q, h=h: land_small.at[which, h, way, q],
            )
            for h in HALVES
        ]
        return first, second

    def add_big(into, term):
        def step(j, carry):
            into[j] = (into[j].astype(F32) + term[j].astype(F32)).astype(BF16)
            return carry

        lax.fori_loop(0, SIDE, step, 0)

    def add_small(into, term):
        into[...] = (into[...].astype(F32) + term[...].astype(F32)).astype(BF16)

    def close_first(rows, which, h):
        mine = place.outer(h)

        def step(j, carry):
            for q in PIECES:
                total = rows[h, q, mine, j].astype(F32)
                for way in (0, 1):
                    total += land_big[which, h, way, q, j].astype(F32)
                rows[h, q, mine, j] = total.astype(BF16)
            return carry

        lax.fori_loop(0, SIDE, step, 0)

    first_o, second_o = reduces(part, 0)
    first_b, second_b = reduces(rows_x, 1)

    for h in HALVES:
        first_o[h].start()

    for h in HALVES:
        second_g[h].finish()

    def unit_grads(z, carry):
        here = pl.ds(pl.multiple_of(z * group, group), group)
        hidden_grad = jnp.zeros((group, units), F32)
        for h, q in CORNERS:
            hidden_grad += dot_nt(block_rows(rows_g, h, q, z), down_w[:, span(h, q)])
        gate = pre_g[here, :]
        sigma = jax.nn.sigmoid(gate)
        grad_g[here, :] = (
            hidden_grad * pre_u[here, :] * (sigma * (1.0 + gate * (1.0 - sigma)))
        ).astype(BF16)
        grad_u[here, :] = (hidden_grad * (gate * sigma)).astype(BF16)
        return carry

    lax.fori_loop(0, SIDE, unit_grads, 0)

    for h in HALVES:
        first_o[h].relay(add_big)

    for rings in (first_x, second_x):
        for h in HALVES:
            rings[h].wait_sends()

    def backward_terms(z, carry):
        here = pl.ds(pl.multiple_of(z * group, group), group)
        gate_here, up_here = grad_g[here, :], grad_u[here, :]
        for h, q in CORNERS:
            term = dot_nt(gate_here, gate_w[span(h, q), :])
            put_rows(rows_x, h, q, z, term + dot_nt(up_here, up_w[span(h, q), :]))
        return carry

    lax.fori_loop(0, SIDE, backward_terms, 0)

    for h in HALVES:
        first_b[h].start_far()

    local_pick, local_share = selection(info[0])

    def close_second(rows, which, h, q, staged):
        total = rows[h, q, place.outer(h), place.inner(h)].astype(F32)
        for way in (0, 1):
            total += land_small[which, h, way, q].astype(F32)
        if which == 0:
            total = total * local_share
        spread = lax.dot_general(
            local_pick, total.astype(BF16), (((0,), (0,)), ((), ())), preferred_element_type=F32
        )
        down_w[pl.ds(staged, toks), span(h, q)] = spread.astype(BF16)

    def close(rows, which, second):
        for h in HALVES:
            second[h].finish()
            for q in PIECES:
                close_second(rows, which, h, q, which * toks)

    for h in HALVES:
        first_o[h].finish()
        close_first(part, 0, h)
        second_o[h].start()
    for h in HALVES:
        first_b[h].start_near()
    for h in HALVES:
        first_b[h].relay(add_big)
    for h in HALVES:
        second_o[h].relay(add_small)
    close(part, 0, second_o)
    store_out = pltpu.make_async_copy(acts_here, out_ref, store_sem.at[0])
    store_out.start()
    for h in HALVES:
        first_b[h].finish()
        close_first(rows_x, 1, h)
        second_b[h].start()
    for h in HALVES:
        second_b[h].relay(add_small)
    close(rows_x, 1, second_b)
    store_grad = pltpu.make_async_copy(cots_here, grad_ref, store_sem.at[1])
    store_grad.start()

    info_back.wait_send()
    info_on.wait_send()
    for rings in (first_g, second_g, first_o, second_o, first_b, second_b):
        for h in HALVES:
            rings[h].wait_sends()
    store_out.wait()
    store_grad.wait()
    assert links.used == COPIES


COPIES = 2 + 8 + 2 * 4 * 6 + 2 * 4 * 6


def body(sections, sent_acts, sent_cots, expert_ids, gate_probs, gate_weight, up_weight, down_weight):
    acts, cots = sent_acts[0], sent_cots[0]
    ids, probs = expert_ids[0].T, gate_probs[0].T
    toks, width = acts.shape
    cols = width // 4
    units = gate_weight.shape[2]
    rows = SIDE * SIDE * CAP
    hbm = pl.BlockSpec(memory_space=pl.ANY)
    vmem = pl.BlockSpec(memory_space=pltpu.VMEM)
    block = (CAP, cols)
    out_acts, in_grads = pl.pallas_call(
        functools.partial(kernel, sections),
        out_shape=(
            jax.ShapeDtypeStruct((toks, width), BF16),
            jax.ShapeDtypeStruct((toks, width), BF16),
        ),
        in_specs=[hbm, hbm, vmem, vmem, hbm, hbm, hbm],
        out_specs=(hbm, hbm),
        scratch_shapes=[
            pltpu.VMEM((width, units), BF16),
            pltpu.VMEM((width, units), BF16),
            pltpu.VMEM((units, width), BF16),
            pltpu.VMEM((3, 8, toks), F32),
            pltpu.VMEM((2, 2, SIDE, SIDE) + block, BF16),
            pltpu.VMEM((2, 2, SIDE, SIDE) + block, BF16),
            pltpu.VMEM((2, 2, SIDE, SIDE) + block, BF16),
            pltpu.VMEM((rows, units), F32),
            pltpu.VMEM((rows, units), F32),
            pltpu.VMEM((rows, units), BF16),
            pltpu.VMEM((rows, units), BF16),
            pltpu.VMEM((rows, units), BF16),
            pltpu.VMEM((2, 2, 2, SIDE) + block, BF16),
            pltpu.VMEM((2, 2, 2, 2, SIDE) + block, BF16),
            pltpu.VMEM((2, 2, 2) + block, BF16),
            pltpu.VMEM((2, 2, 2, 2) + block, BF16),
            pltpu.SemaphoreType.DMA((COPIES,)),
            pltpu.SemaphoreType.DMA((COPIES,)),
            pltpu.SemaphoreType.DMA((5,)),
            pltpu.SemaphoreType.DMA((2,)),
        ],
        compiler_params=pltpu.CompilerParams(
            collective_id=0, has_side_effects=True, vmem_limit_bytes=67043328
        ),
    )(acts, cots, ids, probs, gate_weight[0], up_weight[0], down_weight[0])
    return (out_acts[None], in_grads[None])


def solution(mesh):
    placed = (
        P("section", "expert", None),
        P("section", "expert", None),
        P("section", "expert", None),
        P("section", "expert", None),
        P("section", None, "expert"),
        P("section", None, "expert"),
        P("section", "expert", None),
    )
    return jax.shard_map(
        functools.partial(body, mesh.shape["section"]),
        mesh=mesh,
        in_specs=placed,
        out_specs=(P("section", "expert", None), P("section", "expert", None)),
        check_vma=False,
    )
```

```python
import functools

import jax
import jax.numpy as jnp
from jax import lax
from jax.experimental import pallas as pl
from jax.experimental.pallas import tpu as pltpu
from jax.sharding import PartitionSpec as P

CAP = 40
SIDE = 4
MESH = pl.DeviceIdType.MESH
F32 = jnp.float32
BF16 = jnp.bfloat16
HALVES = (0, 1)
PIECES = (0, 1)
CORNERS = ((0, 0), (1, 0), (0, 1), (1, 1))


def dot_nn(lhs, rhs):
    return lax.dot_general(lhs, rhs, (((1,), (0,)), ((), ())), preferred_element_type=F32)


def dot_nt(lhs, rhs):
    return lax.dot_general(lhs, rhs, (((1,), (1,)), ((), ())), preferred_element_type=F32)


def routing(ids, probs):
    toks = ids.shape[1]
    chosen = ids == 0
    flags = jnp.where(chosen, 1.0, 0.0).astype(F32)
    weights = jnp.where(chosen, probs, 0.0)
    picked = jnp.broadcast_to(flags[0:1] + flags[1:2], (8, toks))
    share = jnp.broadcast_to(weights[0:1] + weights[1:2], (8, toks))
    earlier = lax.broadcasted_iota(jnp.int32, (toks, toks), 0) < lax.broadcasted_iota(
        jnp.int32, (toks, toks), 1
    )
    rank = dot_nn(picked.astype(BF16), jnp.where(earlier, 1.0, 0.0).astype(BF16))
    slot = jnp.where(picked > 0.5, rank, -1.0)
    line = lax.broadcasted_iota(jnp.int32, (8, toks), 0)
    return jnp.where(line == 0, slot, share)


def selection(toks, block):
    slot_line = block[0:1, :]
    share_line = block[1:2, :]
    number = lax.broadcasted_iota(jnp.int32, (CAP, toks), 0).astype(F32)
    hit = number == slot_line
    pick = jnp.where(hit, 1.0, 0.0).astype(BF16)
    slot_share = jnp.sum(jnp.where(hit, share_line, 0.0), axis=1, keepdims=True)
    return pick, slot_share


class Place:
    def __init__(self, sections):
        self.sections = sections
        self.section = lax.axis_index("section")
        self.expert = lax.axis_index("expert")
        self.at = (self.expert // SIDE, self.expert % SIDE)

    def axis(self, half, phase):
        return 1 - half if phase == 1 else half

    def beside(self, axis, step):
        z, y = self.at
        if axis == 0:
            z = (z + step) % SIDE
        else:
            y = (y + step) % SIDE
        return (self.section, z * SIDE + y)

    def other_section(self, step):
        return ((self.section + step) % self.sections, self.expert)

    def outer(self, half):
        return self.at[half]

    def inner(self, half):
        return self.at[1 - half]


class Links:
    def __init__(self, send_sem, recv_sem):
        self.send_sem, self.recv_sem = send_sem, recv_sem
        self.used = 0

    def copy(self, src, dst, device):
        k = self.used
        self.used += 1
        return pltpu.make_async_remote_copy(
            src_ref=src,
            dst_ref=dst,
            send_sem=self.send_sem.at[k],
            recv_sem=self.recv_sem.at[k],
            device_id=device,
            device_id_type=MESH,
        )


class GatherRing:
    def __init__(self, place, links, half, phase, piece):
        axis = place.axis(half, phase)
        me = place.at[axis]
        plus, minus = place.beside(axis, 1), place.beside(axis, SIDE - 1)
        before, after = (me + SIDE - 1) % SIDE, (me + 1) % SIDE
        self.own = [
            [links.copy(piece(q, me), piece(q, me), device) for device in (plus, minus)]
            for q in PIECES
        ]
        self.passed = [
            links.copy(piece(0, before), piece(0, before), plus),
            links.copy(piece(1, after), piece(1, after), minus),
        ]

    def start(self, q):
        self.own[q][q].start()
        self.own[q][1 - q].start()

    def relay(self):
        for q in PIECES:
            self.own[q][q].wait_recv()
            self.passed[q].start()

    def finish(self):
        self.own[0][1].wait_recv()
        self.own[1][0].wait_recv()
        self.passed[0].wait_recv()
        self.passed[1].wait_recv()

    def wait_sends(self):
        for q in PIECES:
            for way in (0, 1):
                self.own[q][way].wait_send()
            self.passed[q].wait_send()


class ReduceRing:
    def __init__(self, place, links, half, phase, piece, through, landed):
        axis = place.axis(half, phase)
        me = place.at[axis]
        plus, minus = place.beside(axis, 1), place.beside(axis, SIDE - 1)
        before, after = (me + SIDE - 1) % SIDE, (me + 1) % SIDE
        opposite = (me + 2) % SIDE
        self.piece, self.me, self.through, self.landed = piece, me, through, landed
        self.next = (after, before)
        devices = (plus, minus)
        self.far = [links.copy(piece(q, opposite), through(q), devices[q]) for q in PIECES]
        self.near = [
            links.copy(piece(1 - q, self.next[q]), landed(q, 1 - q), devices[q]) for q in PIECES
        ]
        self.passed = [links.copy(through(q), landed(q, q), devices[q]) for q in PIECES]

    def start_far(self):
        for q in PIECES:
            self.far[q].start()

    def start_near(self):
        for q in PIECES:
            self.near[q].start()

    def start(self):
        self.start_far()
        self.start_near()

    def relay(self, add_into):
        for q in PIECES:
            self.far[q].wait_recv()
            add_into(self.through(q), self.piece(q, self.next[q]))
            self.passed[q].start()

    def finish(self):
        for q in PIECES:
            self.near[q].wait_recv()
            self.passed[q].wait_recv()

    def wait_sends(self):
        for q in PIECES:
            self.far[q].wait_send()
            self.near[q].wait_send()
            self.passed[q].wait_send()


def kernel(
    sections,
    acts_ref,
    cots_ref,
    ids_ref,
    probs_ref,
    gate_ref,
    up_ref,
    down_ref,
    slots_ref,
    gate_w,
    up_w,
    down_w,
    info,
    rows_x,
    rows_g,
    part,
    pre_g,
    pre_u,
    hid,
    grad_g,
    grad_u,
    thru_big,
    land_big,
    thru_small,
    land_small,
    send_sem,
    recv_sem,
    load_sem,
):
    place = Place(sections)
    links = Links(send_sem, recv_sem)
    toks, width = acts_ref.shape
    cols = width // 4
    units = gate_ref.shape[1]
    group = SIDE * CAP

    def span(h, q):
        return pl.ds((h * 2 + q) * cols, cols)

    barrier = pltpu.get_barrier_semaphore()
    around = [place.beside(axis, step) for axis in (0, 1) for step in (1, SIDE - 1)]
    around += [place.other_section(step) for step in (1, sections - 1)]
    for device in around:
        pl.semaphore_signal(barrier, inc=1, device_id=device, device_id_type=MESH)

    acts_here = down_w.at[pl.ds(0, toks)]
    cots_here = down_w.at[pl.ds(toks, toks)]
    load_acts = pltpu.make_async_copy(acts_ref, acts_here, load_sem.at[0])
    load_cots = pltpu.make_async_copy(cots_ref, cots_here, load_sem.at[1])
    load_gate = pltpu.make_async_copy(gate_ref, gate_w, load_sem.at[2])
    load_up = pltpu.make_async_copy(up_ref, up_w, load_sem.at[3])
    load_down = pltpu.make_async_copy(down_ref, down_w, load_sem.at[4])
    load_acts.start()
    load_cots.start()

    info[0] = routing(ids_ref[...], probs_ref[...])

    pl.semaphore_wait(barrier, len(around))
    info_back = links.copy(info.at[0], info.at[1], place.other_section(sections - 1))
    info_on = links.copy(info.at[0], info.at[2], place.other_section(1))
    info_back.start()
    info_on.start()

    def own_slot(rows, h, q):
        return rows.at[h, q, place.outer(h), place.inner(h)]

    load_acts.wait()
    info_back.wait_recv()
    pick, _ = selection(toks, info[1])
    send_x = {}
    for h, q in CORNERS:
        part[h, q, 0, 0] = dot_nn(pick, down_w[pl.ds(0, toks), span(h, q)]).astype(BF16)
        send_x[h, q] = links.copy(
            part.at[h, q, 0, 0], own_slot(rows_x, h, q), place.other_section(1)
        )
        send_x[h, q].start()

    load_cots.wait()
    info_on.wait_recv()
    pick, slot_share = selection(toks, info[2])
    send_g = {}
    for h, q in CORNERS:
        chosen_rows = dot_nn(pick, down_w[pl.ds(toks, toks), span(h, q)])
        part[h, q, 0, 1] = (chosen_rows * slot_share).astype(BF16)
        send_g[h, q] = links.copy(
            part.at[h, q, 0, 1], own_slot(rows_g, h, q), place.other_section(sections - 1)
        )
        send_g[h, q].start()

    load_gate.start()
    load_up.start()
    load_down.start()

    def gathers(rows):
        first = [
            GatherRing(place, links, h, 1, lambda q, j, h=h: rows.at[h, q, place.outer(h), j])
            for h in HALVES
        ]
        second = [
            GatherRing(place, links, h, 2, lambda q, j, h=h: rows.at[h, q, j]) for h in HALVES
        ]
        return first, second

    first_x, second_x = gathers(rows_x)
    first_g, second_g = gathers(rows_g)

    for h, q in CORNERS:
        send_x[h, q].wait_recv()
        first_x[h].start(q)
    for h, q in CORNERS:
        send_g[h, q].wait_recv()
        first_g[h].start(q)
    for h in HALVES:
        first_x[h].relay()
    for h in HALVES:
        first_x[h].finish()
        for q in PIECES:
            second_x[h].start(q)
    for h in HALVES:
        first_g[h].relay()
    for h in HALVES:
        second_x[h].relay()
    for h in HALVES:
        first_g[h].finish()
        for q in PIECES:
            second_g[h].start(q)
    for h in HALVES:
        second_x[h].finish()

    def block_rows(rows, h, q, z):
        value = rows[h, q, z] if h == 0 else rows[h, q, :, z]
        return value.reshape(group, cols)

    def put_rows(rows, h, q, z, value):
        value = value.astype(BF16).reshape(SIDE, CAP, cols)
        if h == 0:
            rows[h, q, z] = value
        else:
            rows[h, q, :, z] = value

    load_gate.wait()
    load_up.wait()

    def project(z, carry):
        here = pl.ds(pl.multiple_of(z * group, group), group)
        total_g = jnp.zeros((group, units), F32)
        total_u = jnp.zeros((group, units), F32)
        for h, q in CORNERS:
            block = block_rows(rows_x, h, q, z)
            total_g += dot_nn(block, gate_w[span(h, q), :])
            total_u += dot_nn(block, up_w[span(h, q), :])
        pre_g[here, :] = total_g
        pre_u[here, :] = total_u
        hid[here, :] = (total_g * jax.nn.sigmoid(total_g) * total_u).astype(BF16)
        return carry

    lax.fori_loop(0, SIDE, project, 0)

    for h in HALVES:
        second_g[h].relay()

    load_down.wait()
    for h, q in CORNERS:
        send_x[h, q].wait_send()
        send_g[h, q].wait_send()

    def forward_terms(z, carry):
        here = pl.ds(pl.multiple_of(z * group, group), group)
        units_here = hid[here, :]
        for h, q in CORNERS:
            put_rows(part, h, q, z, dot_nn(units_here, down_w[:, span(h, q)]))
        return carry

    lax.fori_loop(0, SIDE, forward_terms, 0)

    def second_sums(rows, which):
        return [
            ReduceRing(
                place,
                links,
                h,
                1,
                lambda q, j, h=h: rows.at[h, q, place.outer(h), j],
                lambda q, h=h: thru_small.at[which, h, q],
                lambda way, q, h=h: land_small.at[which, h, way, q],
            )
            for h in HALVES
        ]

    first_o = [
        ReduceRing(
            place,
            links,
            h,
            2,
            lambda q, j, h=h: part.at[h, q, j],
            lambda q, h=h: thru_big.at[0, h, q],
            lambda way, q, h=h: land_big.at[0, h, way, q],
        )
        for h in HALVES
    ]
    second_o = second_sums(part, 0)

    def block_of(h, n):
        return (place.inner(h) + (2, 1, 3, 0)[n]) % SIDE

    first_b = [
        [
            ReduceRing(
                place,
                links,
                h,
                2,
                lambda q, j, h=h, n=n: rows_x.at[h, q, j, block_of(h, n)],
                lambda q, h=h, n=n: thru_big.at[1, h, q, n],
                lambda way, q, h=h, n=n: land_big.at[1, h, way, q, n],
            )
            for h in HALVES
        ]
        for n in range(SIDE)
    ]
    second_b = second_sums(rows_x, 1)

    def add_big(into, term):
        def step(j, carry):
            into[j] = (into[j].astype(F32) + term[j].astype(F32)).astype(BF16)
            return carry

        lax.fori_loop(0, SIDE, step, 0)

    def add_small(into, term):
        into[...] = (into[...].astype(F32) + term[...].astype(F32)).astype(BF16)

    def close_block(rows, which, h, j, n):
        mine = place.outer(h)
        for q in PIECES:
            total = rows[h, q, mine, j].astype(F32)
            for way in (0, 1):
                total += land_big[which, h, way, q, n].astype(F32)
            rows[h, q, mine, j] = total.astype(BF16)

    def close_first(h):
        def step(j, carry):
            close_block(part, 0, h, j, j)
            return carry

        lax.fori_loop(0, SIDE, step, 0)

    for h in HALVES:
        first_o[h].start()

    for h in HALVES:
        second_g[h].finish()

    def unit_grads(z, carry):
        here = pl.ds(pl.multiple_of(z * group, group), group)
        hidden_grad = jnp.zeros((group, units), F32)
        for h, q in CORNERS:
            hidden_grad += dot_nt(block_rows(rows_g, h, q, z), down_w[:, span(h, q)])
        gate = pre_g[here, :]
        sigma = jax.nn.sigmoid(gate)
        grad_g[here, :] = (
            hidden_grad * pre_u[here, :] * (sigma * (1.0 + gate * (1.0 - sigma)))
        ).astype(BF16)
        grad_u[here, :] = (hidden_grad * (gate * sigma)).astype(BF16)
        return carry

    lax.fori_loop(0, SIDE, unit_grads, 0)

    for h in HALVES:
        first_o[h].relay(add_big)

    for rings in (first_x, second_x):
        for h in HALVES:
            rings[h].wait_sends()

    def backward_terms(z, carry):
        here = pl.ds(pl.multiple_of(z * group, group), group)
        gate_here, up_here = grad_g[here, :], grad_u[here, :]
        for h, q in CORNERS:
            term = dot_nt(gate_here, gate_w[span(h, q), :])
            put_rows(rows_x, h, q, z, term + dot_nt(up_here, up_w[span(h, q), :]))
        return carry

    lax.fori_loop(0, SIDE, backward_terms, 0)

    for rings in first_b:
        for h in HALVES:
            rings[h].start_far()

    _, local_share = selection(toks, info[0])

    def close_second(rows, which, h, q):
        total = rows[h, q, place.outer(h), place.inner(h)].astype(F32)
        for way in (0, 1):
            total += land_small[which, h, way, q].astype(F32)
        if which == 0:
            total = total * local_share
        slots_ref[which, :, span(h, q)] = total.astype(BF16)

    def close(rows, which, second):
        for h in HALVES:
            second[h].finish()
            for q in PIECES:
                close_second(rows, which, h, q)

    def pass_block(n):
        for h in HALVES:
            first_b[n][h].start_near()
        for h in HALVES:
            first_b[n][h].relay(add_small)

    def finish_block(n, h):
        first_b[n][h].finish()
        close_block(rows_x, 1, h, block_of(h, n), n)

    for h in HALVES:
        first_o[h].finish()
        close_first(h)
        second_o[h].start()
    pass_block(0)
    pass_block(1)
    for h in HALVES:
        second_o[h].relay(add_small)
    pass_block(2)
    for h in HALVES:
        finish_block(0, h)
        second_b[h].start_far()
    for h in HALVES:
        finish_block(1, h)
        second_b[h].near[0].start()
    pass_block(3)
    for h in HALVES:
        finish_block(2, h)
        second_b[h].near[1].start()
    for h in HALVES:
        second_b[h].relay(add_small)
    close(part, 0, second_o)
    for h in HALVES:
        finish_block(3, h)
    close(rows_x, 1, second_b)

    info_back.wait_send()
    info_on.wait_send()
    for rings in (first_g, second_g, first_o, second_o, *first_b, second_b):
        for h in HALVES:
            rings[h].wait_sends()
    assert links.used == COPIES


def spread_kernel(slots_ref, ids_ref, probs_ref, out_ref, grad_ref, staged, store_sem):
    toks, width = out_ref.shape
    cols = width // 4
    pick, _ = selection(toks, routing(ids_ref[...], probs_ref[...]))
    stores = []
    for which, target in enumerate((out_ref, grad_ref)):
        for k in range(4):
            here = pl.ds(k * cols, cols)
            spread = lax.dot_general(
                pick, slots_ref[which, :, here], (((0,), (0,)), ((), ())), preferred_element_type=F32
            )
            staged[which, k] = spread.astype(BF16)
            store = pltpu.make_async_copy(
                staged.at[which, k], target.at[:, here], store_sem.at[which, k]
            )
            store.start()
            stores.append(store)
    for store in stores:
        store.wait()


COPIES = 2 + 8 + 2 * 4 * 6 + 2 * 2 * 6 + 2 * 5 * 6


def body(sections, sent_acts, sent_cots, expert_ids, gate_probs, gate_weight, up_weight, down_weight):
    acts, cots = sent_acts[0], sent_cots[0]
    ids, probs = expert_ids[0].T, gate_probs[0].T
    toks, width = acts.shape
    cols = width // 4
    units = gate_weight.shape[2]
    rows = SIDE * SIDE * CAP
    hbm = pl.BlockSpec(memory_space=pl.ANY)
    vmem = pl.BlockSpec(memory_space=pltpu.VMEM)
    block = (CAP, cols)
    slots = pl.pallas_call(
        functools.partial(kernel, sections),
        out_shape=pltpu.VMEM((2, CAP, width), BF16),
        in_specs=[hbm, hbm, vmem, vmem, hbm, hbm, hbm],
        out_specs=vmem,
        scratch_shapes=[
            pltpu.VMEM((width, units), BF16),
            pltpu.VMEM((width, units), BF16),
            pltpu.VMEM((units, width), BF16),
            pltpu.VMEM((3, 8, toks), F32),
            pltpu.VMEM((2, 2, SIDE, SIDE) + block, BF16),
            pltpu.VMEM((2, 2, SIDE, SIDE) + block, BF16),
            pltpu.VMEM((2, 2, SIDE, SIDE) + block, BF16),
            pltpu.VMEM((rows, units), F32),
            pltpu.VMEM((rows, units), F32),
            pltpu.VMEM((rows, units), BF16),
            pltpu.VMEM((rows, units), BF16),
            pltpu.VMEM((rows, units), BF16),
            pltpu.VMEM((2, 2, 2, SIDE) + block, BF16),
            pltpu.VMEM((2, 2, 2, 2, SIDE) + block, BF16),
            pltpu.VMEM((2, 2, 2) + block, BF16),
            pltpu.VMEM((2, 2, 2, 2) + block, BF16),
            pltpu.SemaphoreType.DMA((COPIES,)),
            pltpu.SemaphoreType.DMA((COPIES,)),
            pltpu.SemaphoreType.DMA((5,)),
        ],
        compiler_params=pltpu.CompilerParams(
            collective_id=0, has_side_effects=True, vmem_limit_bytes=63000000
        ),
    )(acts, cots, ids, probs, gate_weight[0], up_weight[0], down_weight[0])
    out_acts, in_grads = pl.pallas_call(
        spread_kernel,
        out_shape=(
            jax.ShapeDtypeStruct((toks, width), BF16),
            jax.ShapeDtypeStruct((toks, width), BF16),
        ),
        in_specs=[vmem, vmem, vmem],
        out_specs=(hbm, hbm),
        scratch_shapes=[
            pltpu.VMEM((2, 4, toks, cols), BF16),
            pltpu.SemaphoreType.DMA((2, 4)),
        ],
        compiler_params=pltpu.CompilerParams(vmem_limit_bytes=8 << 20),
    )(slots, ids, probs)
    return (out_acts[None], in_grads[None])


def solution(mesh):
    placed = (
        P("section", "expert", None),
        P("section", "expert", None),
        P("section", "expert", None),
        P("section", "expert", None),
        P("section", None, "expert"),
        P("section", None, "expert"),
        P("section", "expert", None),
    )
    return jax.shard_map(
        functools.partial(body, mesh.shape["section"]),
        mesh=mesh,
        in_specs=placed,
        out_specs=(P("section", "expert", None), P("section", "expert", None)),
        check_vma=False,
    )
```
